32 devices in a mesh: dp: 8 (over z, x), seq: 4 (over y, core).
Axes of the slice: x: 2, y: 2, z: 4, core: 2. Of those that a mesh axis runs over, the one named last changes fastest.
Arguments:
- patches: bfloat16 [32, 12288], P(None, ('dp', 'seq')), may hold values from -12 to 12
- segment_ids: int32 [8, 1536], P('dp'), may hold values from 0 to 15, never falling along the last dimension, each value on 1 to 1152 neighbouring positions
- regroup_plan: int32 [8, 5, 16], P('dp'), may hold values from 0 to 383, as said below
- input_weight: bfloat16 [32, 1280], replicated, may hold values from -1 to 1
- input_bias: float32 [1280], replicated, may hold values from -3 to 3
- skip_weight: bfloat16 [32, 1280], replicated, may hold values from -1 to 1
- hidden_weight: bfloat16 [1280, 1280], replicated, may hold values from -0.15625 to 0.15625
- output_bias: float32 [1280], replicated, may hold values from -3 to 3
- norm_gain: float32 [1280], replicated, may hold values from 0.1 to 1.9
- head_scale: float32 [8], replicated, may hold values from 1 to 4
- qkv_weight: bfloat16 [1280, 3, 640], replicated, may hold values from -0.15625 to 0.15625
- out_weight: bfloat16 [640, 1280], P(None, ('dp', 'seq')), may hold values from -0.25 to 0.25
- cotangent: bfloat16 [12288, 1280], P(('dp', 'seq')), may hold values from -0.4375 to 0.4375
Outputs:
- layer_out: bfloat16 [12288, 1280], P(('dp', 'seq'))
- out_grad: float32 [640, 1280], P(None, ('dp', 'seq'))
The draws below stay inside these ranges and needn't reach their ends.
Inputs may be any that keep to these rules, and one draw needn't show every extreme that they name: `regroup_plan`: piece s * 4 + d of a window moves rows of source shard s to destination shard d: one piece for each pair, each moving one row or more. The pieces of a window cover each of the 384 rows of every source shard once and each of the 384 rows of every destination shard once. A piece moves at most 192 rows, and in every window some piece moves exactly 192. `segment_ids`: series ids never fall along a window's positions; one series of each window has exactly 1152 positions.
All inputs are finite; a program needn't handle non-finite values.
Results may differ from the reference program's by a relative error of at most 0.015.
Values may be sent and summed in bfloat16 or wider, within the bound.
No kernel may reach another device: no remote copies, remote signals or barrier semaphores. Data moves between devices by JAX's collectives and lax.ppermute only.
A program may use at most 64 MiB of HBM per device.

```python
import math
import jax
import jax.numpy as jnp
import numpy as np
from jax import lax

D = 1280
FF = 1280
PATCH = 32
HD = 80
HEADS = 8
HW = 640
ROWS_DEV = 384
SEGS = 16
SHARDS = 4
WINDOW_LEN = 1536
MOST = 1152
WINDOWS = 8
TOKENS = 12288


def random_order(sub_key):
    return jax.random.permutation(sub_key, SHARDS)


def window_pieces(seed_key):
    shard_count = SHARDS
    unit_rows = ROWS_DEV // SHARDS
    first_key, second_key, third_key, fourth_key, fifth_key = jax.random.split(seed_key, 5)
    chosen = jax.random.permutation(first_key, shard_count)
    moved = jax.random.randint(second_key, (), 1, unit_rows)
    shares = jnp.full((shard_count,), unit_rows, jnp.int32)
    shares = shares.at[chosen[0]].add(unit_rows).at[chosen[1]].add(-moved).at[chosen[2]].add(moved - unit_rows)
    taker_perm = jax.random.permutation(fifth_key, shard_count)
    sender = jnp.broadcast_to(jnp.arange(shard_count, dtype=jnp.int32)[:, None], (shard_count, shard_count))
    taker = jnp.broadcast_to(jnp.arange(shard_count, dtype=jnp.int32)[None, :], (shard_count, shard_count))
    counts = shares[(taker_perm[taker] - sender) % shard_count]
    send_rank = jnp.argsort(jax.vmap(random_order)(jax.random.split(third_key, shard_count)), axis=1)
    first_rows = jnp.sum(jnp.where(send_rank[:, None, :] < send_rank[:, :, None], counts[:, None, :], 0), axis=2)
    take_rank = jnp.argsort(jax.vmap(random_order)(jax.random.split(fourth_key, shard_count)), axis=1)
    by_taker = jnp.transpose(counts)
    offsets = jnp.transpose(jnp.sum(jnp.where(take_rank[:, None, :] < take_rank[:, :, None], by_taker[:, None, :], 0), axis=2))
    fields = jnp.stack([sender, first_rows, counts, taker, offsets])
    return fields.reshape(5, shard_count * shard_count).astype(jnp.int32)


def draw_regroup_plan(key, part):
    return jax.vmap(window_pieces)(jax.random.split(jax.random.fold_in(key, 11), WINDOWS))


def draw_patches(key, part):
    scale_key, value_key = jax.random.split(jax.random.fold_in(key, 7))
    scales = jnp.exp(jax.random.uniform(scale_key, (1, TOKENS), jnp.float32, math.log(0.3), math.log(3.0)))
    raw_values = jnp.clip(jax.random.normal(value_key, (PATCH, TOKENS), jnp.float32), -4.0, 4.0)
    return (raw_values * scales).astype(jnp.bfloat16)


def spiked(result, own_key, source, target, parts, factor):
    def block_of(dim):
        return (jnp.arange(result.shape[dim]) // (result.shape[dim] // parts)).reshape((-1,) + (1,) * (result.ndim - 1 - dim))

    near = jax.random.permutation(own_key, parts)[block_of(target)]
    second = (block_of(target) + parts // 2) % parts
    return jnp.where((block_of(source) == near) | (block_of(source) == second), factor * result, result)


def levels(own_key, dims, cuts, least, high):
    level = 1.0
    for dim, blocks in cuts:
        draws = jax.random.uniform(jax.random.fold_in(jax.random.fold_in(own_key, 6), dim), (blocks,), jnp.float32, least / len(cuts), high / len(cuts))
        level = level * jnp.repeat(jnp.exp(draws), dims[dim] // blocks).reshape((-1,) + (1,) * (len(dims) - 1 - dim))
    return level


def split_up(count, total, limit, skew):
    portions = [(1 << 20) // math.isqrt(standing ** skew) + 1 for standing in range(2, count + 1)]
    spare, given = total - limit - (count - 1), [1] * (count - 1)
    while spare > 0:
        candidates = [i for i in range(count - 1) if given[i] < limit]
        whole, budget = sum([portions[i] for i in candidates]), spare
        for i in candidates:
            addition = min(limit - given[i], max(1, budget * portions[i] // whole), spare)
            given[i] = given[i] + addition
            spare = spare - addition
    return np.array([limit] + given)


def uneven_parts(key, number_of, total, bound, skew):
    if number_of == 2:
        one = jax.random.randint(key, (), max(1, total - bound), min(bound, total - 1) + 1)
        return jnp.stack([one, total - one])
    sizes = jnp.asarray(split_up(number_of, total, bound, skew), jnp.int32)
    twos = (number_of - 1) // 2
    source_of, sink = sizes[1:1 + 2 * twos:2], sizes[2:2 + 2 * twos:2]
    room = jnp.minimum(source_of - 1, bound - sink)
    passed = jax.random.randint(jax.random.fold_in(key, 1), (twos,), 0, 1 << 20) % (room + 1)
    sizes = sizes.at[1:1 + 2 * twos:2].set(source_of - passed).at[2:2 + 2 * twos:2].set(sink + passed)
    return sizes[jax.random.permutation(jax.random.fold_in(key, 2), number_of)]


def bell_draw(key, extent, deviation, most, shards=(), kind=jnp.bfloat16):
    entries = jax.random.normal(key, extent, jnp.float32) * deviation
    if len(shards) > 0:
        entries = levels(key, extent, shards, -0.22, 0.18) * entries
    return jnp.clip(entries, min=-most, max=most).astype(kind)


def heavy_noise(own_key, shape, scale, reach, shards, heavy, kind=jnp.bfloat16):
    result = scale * jax.random.normal(own_key, shape, jnp.float32)
    if shards:
        result = result * levels(own_key, shape, shards, -0.22, 0.18)
    return jnp.clip(spiked(result, jax.random.fold_in(own_key, 3), *heavy), -reach, reach).astype(kind)


def setup_inputs(seed: int = 0) -> dict:
    key_list = jax.random.split(jax.random.key(seed), 14)
    return {
        "patches": draw_patches(jax.random.fold_in(key_list[13], 71), 0),
        "segment_ids": jax.vmap(lambda own: jnp.searchsorted(jnp.cumsum(uneven_parts(own, SEGS, WINDOW_LEN, MOST, 2)), jnp.arange(WINDOW_LEN), side="right"))(jax.random.split(key_list[1], WINDOWS)).reshape((WINDOWS, WINDOW_LEN)).astype(jnp.int32),
        "regroup_plan": draw_regroup_plan(jax.random.fold_in(key_list[13], 71), 0),
        "input_weight": bell_draw(key_list[3], (PATCH, FF), PATCH ** -0.5, 1.0),
        "input_bias": bell_draw(key_list[4], (FF,), 0.5, 3.0, (), jnp.float32),
        "skip_weight": bell_draw(key_list[5], (PATCH, D), PATCH ** -0.5, 1.0),
        "hidden_weight": bell_draw(key_list[6], (FF, D), FF ** -0.5, 0.15625),
        "output_bias": bell_draw(key_list[7], (D,), 0.5, 3.0, (), jnp.float32),
        "norm_gain": jnp.clip(1.0 + 0.18 * jax.random.normal(key_list[8], (D,), jnp.float32), 0.1, 1.9),
        "head_scale": jnp.clip(jnp.exp(jax.random.uniform(key_list[9], (HEADS,), jnp.float32, math.log(1.0), math.log(4.0))), 1.0, 4.0),
        "qkv_weight": bell_draw(key_list[10], (D, 3, HW), D ** -0.5, 0.15625),
        "out_weight": bell_draw(key_list[11], (HW, D), HW ** -0.5, 0.25, ((1, 32),)),
        "cotangent": heavy_noise(key_list[12], (TOKENS, D), (4.0 * TOKENS ** -0.5), 0.4375, ((0, 32),), (0, 1, 32, 2.75)),
    }


EPSILON = 1e-06
CONTRACT_FIRST = (((0,), (0,)), ((), ()))

def row_norm(values):
    return values * lax.rsqrt(lax.optimization_barrier(jnp.mean(values * values, axis=-1, keepdims=True)) + EPSILON)

def round_half(values):
    return lax.optimization_barrier(values.astype(jnp.bfloat16)).astype(jnp.float32)

def place_table(plan_rows, shard_rows, shard_count):
    source = plan_rows[0]
    first_row = plan_rows[1]
    row_count = plan_rows[2]
    target = plan_rows[3]
    offset_row = plan_rows[4]
    window_len = shard_rows * shard_count
    loader_row = jnp.arange(window_len, dtype=jnp.int32)
    begin_row = source * shard_rows + first_row
    inside = (loader_row[None, :] >= begin_row[:, None]) & (loader_row[None, :] < (begin_row + row_count)[:, None])
    earlier = (source[:, None] == source[None, :]) & (target[:, None] == target[None, :]) & (first_row[None, :] < first_row[:, None])
    base_rank = lax.optimization_barrier(jnp.sum(jnp.where(earlier, row_count[None, :], 0), axis=1)).astype(jnp.int32)
    position = lax.optimization_barrier(jnp.sum(jnp.where(inside, (target * shard_rows + offset_row - begin_row)[:, None] + loader_row[None, :], 0), axis=0))
    slot_rank = lax.optimization_barrier(jnp.sum(jnp.where(inside, (base_rank - begin_row)[:, None] + loader_row[None, :], 0), axis=0))
    return (position.astype(jnp.int32), slot_rank.astype(jnp.int32))

def patch_block(columns, input_weight, input_bias, skip_weight, hidden_weight, output_bias):
    pre_act = lax.dot_general(columns, input_weight, CONTRACT_FIRST, preferred_element_type=jnp.float32) + input_bias
    hidden = jax.nn.silu(pre_act).astype(jnp.bfloat16)
    skipped = lax.dot_general(columns, skip_weight, CONTRACT_FIRST, preferred_element_type=jnp.float32)
    embedded = jnp.dot(hidden, hidden_weight, preferred_element_type=jnp.float32) + skipped + output_bias
    return embedded.astype(jnp.bfloat16)

def window_attention(projected, segment_row, head_scale):
    queries = round_half(row_norm(projected[:, 0].astype(jnp.float32)))
    key_rows = round_half(row_norm(projected[:, 1].astype(jnp.float32)))
    value_rows = projected[:, 2].astype(jnp.float32)
    block_len = min(512, WINDOW_LEN)
    position = jnp.arange(WINDOW_LEN, dtype=jnp.int32)
    factor = head_scale * (1.0 / math.sqrt(HD))

    def one_block(block_index):
        query_first = block_index * block_len
        query_part = lax.dynamic_slice_in_dim(queries, query_first, block_len, 0)
        scores = jnp.einsum('qhd,khd->hqk', query_part, key_rows) * factor[:, None, None]
        query_pos = query_first + jnp.arange(block_len, dtype=jnp.int32)
        query_seg = lax.dynamic_slice_in_dim(segment_row, query_first, block_len, 0)
        allowed = (query_seg[:, None] == segment_row[None, :]) & (position[None, :] <= query_pos[:, None])
        weights = jnp.where(allowed[None], jnp.exp(scores), 0.0)
        denominator = lax.optimization_barrier(jnp.sum(weights, axis=-1))
        summed = jnp.einsum('hqk,khd->qhd', round_half(weights), value_rows)
        return summed / jnp.transpose(denominator)[:, :, None]
    blocks = lax.map(one_block, jnp.arange(WINDOW_LEN // block_len, dtype=jnp.int32))
    return blocks.reshape(WINDOW_LEN, HW).astype(jnp.bfloat16)

def reference(patches, segment_ids, regroup_plan, input_weight, input_bias, skip_weight, hidden_weight, output_bias, norm_gain, head_scale, qkv_weight, out_weight, cotangent):

    def one_window(grad_sum, window_index):
        first_col = (window_index * WINDOW_LEN).astype(jnp.int32)
        columns = lax.dynamic_slice_in_dim(patches, first_col, WINDOW_LEN, 1)
        embedded = lax.optimization_barrier(patch_block(columns, input_weight, input_bias, skip_weight, hidden_weight, output_bias))
        plan_fields = lax.dynamic_index_in_dim(regroup_plan, window_index, 0, keepdims=False)
        position, slot_rank = place_table(plan_fields, ROWS_DEV, SHARDS)
        inverse = jnp.zeros((WINDOW_LEN,), jnp.int32).at[position].set(jnp.arange(WINDOW_LEN, dtype=jnp.int32))
        ordered = embedded[inverse]
        normed = (row_norm(ordered.astype(jnp.float32)) * norm_gain).astype(jnp.bfloat16)
        projected = jnp.dot(normed, qkv_weight.reshape(D, 3 * HW), preferred_element_type=jnp.float32)
        projected = lax.optimization_barrier(projected.astype(jnp.bfloat16)).reshape(WINDOW_LEN, 3, HEADS, HD)
        segment_row = lax.dynamic_index_in_dim(segment_ids, window_index, 0, keepdims=False)
        attended = window_attention(projected, segment_row, head_scale)
        layer_rows = (ordered.astype(jnp.float32) + jnp.dot(attended, out_weight, preferred_element_type=jnp.float32)).astype(jnp.bfloat16)
        grad_rows = lax.dynamic_slice_in_dim(cotangent, first_col, WINDOW_LEN, 0)
        grad_term = lax.dot_general(attended, grad_rows, CONTRACT_FIRST, preferred_element_type=jnp.float32)
        return (grad_sum + grad_term, layer_rows)
    grad_sum, layer_rows = lax.scan(one_window, jnp.zeros((HW, D), jnp.float32), jnp.arange(WINDOWS, dtype=jnp.int32))
    return (layer_rows.reshape(TOKENS, D), grad_sum)
```

```python
import math

import jax
import jax.numpy as jnp
from jax import lax
from jax.sharding import PartitionSpec as P

HD = 80


EPSILON = 1e-06
CONTRACT_FIRST = (((0,), (0,)), ((), ()))


def row_norm(values):
    return values * lax.rsqrt(jnp.mean(values * values, axis=-1, keepdims=True) + EPSILON)


def bits_down(count):
    bits = []
    step = 1
    while step < count:
        bits.insert(0, step)
        step *= 2
    return bits


def swap(values, axis, step):
    count = lax.axis_size(axis)
    return lax.ppermute(values, axis, [(i, i ^ step) for i in range(count)])


def loader_of_position(plan_rows, shard_rows, shard_count, own):
    source, first_row, row_count, target, offset_row = (plan_rows[i] for i in range(5))
    position = jnp.arange(shard_rows * shard_count, dtype=jnp.int32)
    begin = target * shard_rows + offset_row
    inside = (position[None, :] >= begin[:, None]) & (
        position[None, :] < (begin + row_count)[:, None]
    )
    shift = (source ^ own) * shard_rows + first_row - begin
    return jnp.sum(jnp.where(inside, shift[:, None] + position[None, :], 0), axis=0)


def per_device(
    patches,
    segment_ids,
    regroup_plan,
    input_weight,
    input_bias,
    skip_weight,
    hidden_weight,
    output_bias,
    norm_gain,
    head_scale,
    qkv_weight,
    out_weight,
    cotangent,
):
    shard_count = lax.axis_size("seq")
    group_count = lax.axis_size("dp")
    own = lax.axis_index("seq")
    group = lax.axis_index("dp")
    shard_rows = cotangent.shape[0]
    model_width = cotangent.shape[1]
    window_len = shard_rows * shard_count
    seq_bits = bits_down(shard_count)

    cot = {0: cotangent}
    for step in seq_bits:
        for at in list(cot):
            cot[at ^ step] = swap(cot[at], "seq", step)

    columns = jnp.concatenate(
        [patches] + [swap(patches, "seq", step) for step in range(1, shard_count)], axis=1
    )

    out_rows = jnp.transpose(out_weight)[None]
    order = [0]
    for axis, step, stride in (
        [("seq", step, 1) for step in seq_bits[:-1]]
        + [("dp", step, shard_count) for step in bits_down(group_count)]
        + [("seq", step, 1) for step in seq_bits[-1:]]
    ):
        out_rows = jnp.concatenate([out_rows, swap(out_rows, axis, step)], axis=0)
        order = order + [at ^ (step * stride) for at in order]
    where = [0] * len(order)
    for index, at in enumerate(order):
        where[at] = index
    device = group * shard_count + own
    out_full = out_rows[
        jnp.asarray(where, jnp.int32)[device ^ jnp.arange(len(order), dtype=jnp.int32)]
    ].reshape(model_width, -1)

    loader = loader_of_position(regroup_plan[0], shard_rows, shard_count, own)
    pick = (jnp.arange(window_len, dtype=jnp.int32)[:, None] == loader[None, :]).astype(
        jnp.bfloat16
    )
    chosen = jnp.dot(columns, pick, preferred_element_type=jnp.float32).astype(jnp.bfloat16)
    pre_act = (
        lax.dot_general(chosen, input_weight, CONTRACT_FIRST, preferred_element_type=jnp.float32)
        + input_bias
    )
    hidden = jax.nn.silu(pre_act).astype(jnp.bfloat16)
    skipped = lax.dot_general(
        chosen, skip_weight, CONTRACT_FIRST, preferred_element_type=jnp.float32
    )
    embedded = (
        jnp.dot(hidden, hidden_weight, preferred_element_type=jnp.float32) + skipped + output_bias
    ).astype(jnp.bfloat16)
    normed = (row_norm(embedded.astype(jnp.float32)) * norm_gain).astype(jnp.bfloat16)

    local_width = qkv_weight.shape[2] // shard_count
    local_heads = local_width // HD
    own_qkv = lax.dynamic_slice_in_dim(qkv_weight, own * local_width, local_width, 2)
    projected = jnp.einsum(
        "td,dcw->ctw", normed, own_qkv, preferred_element_type=jnp.float32
    ).astype(jnp.bfloat16)
    heads = projected.reshape(3, window_len, local_heads, HD)
    queries = row_norm(heads[0].astype(jnp.float32)).astype(jnp.bfloat16)
    key_rows = row_norm(heads[1].astype(jnp.float32)).astype(jnp.bfloat16)
    value_rows = heads[2]
    factor = lax.dynamic_slice_in_dim(head_scale, own * local_heads, local_heads, 0) * (
        1.0 / math.sqrt(HD)
    )
    segment_row = segment_ids[0]
    block_len = min(512, window_len)
    pieces = []
    for query_first in range(0, window_len, block_len):
        key_len = query_first + block_len
        query_part = queries[query_first:key_len]
        query_pos = query_first + jnp.arange(block_len, dtype=jnp.int32)
        query_seg = segment_row[query_first:key_len]
        key_seg = segment_row[:key_len]
        key_pos = jnp.arange(key_len, dtype=jnp.int32)
        scores = (
            jnp.einsum(
                "qhd,khd->hqk", query_part, key_rows[:key_len], preferred_element_type=jnp.float32
            )
            * factor[:, None, None]
        )
        allowed = (query_seg[:, None] == key_seg[None, :]) & (
            key_pos[None, :] <= query_pos[:, None]
        )
        weights = jnp.where(allowed[None], jnp.exp(scores), 0.0)
        summed = jnp.einsum(
            "hqk,khd->qhd",
            weights.astype(jnp.bfloat16),
            value_rows[:key_len],
            preferred_element_type=jnp.float32,
        )
        denominator = jnp.sum(weights, axis=-1)
        pieces.append(
            (summed / jnp.transpose(denominator)[:, :, None]).reshape(block_len, local_width)
        )
    attended = jnp.concatenate(pieces, axis=0).astype(jnp.bfloat16)
    by_shard = attended.reshape(shard_count, shard_rows, local_width)
    relative = by_shard[own ^ jnp.arange(shard_count, dtype=jnp.int32)]

    grad = sum(
        lax.dot_general(
            cot[at], relative[at], CONTRACT_FIRST, preferred_element_type=jnp.float32
        )
        for at in range(shard_count)
    )
    blocks = grad.astype(jnp.bfloat16).reshape(group_count, -1, local_width)
    width = group_count
    rev = []
    for index in range(width):
        value, low = 0, index
        for _ in bits_down(width):
            value = value * 2 + low % 2
            low //= 2
        rev.append(value)
    blocks = blocks[group ^ jnp.asarray(rev, jnp.int32)]
    for step in reversed(bits_down(group_count)):
        half = blocks.shape[0] // 2
        blocks = (
            blocks[:half].astype(jnp.float32) + swap(blocks[half:], "dp", step).astype(jnp.float32)
        ).astype(jnp.bfloat16)
    columns_own = blocks.reshape(shard_count, -1, local_width)

    grad_parts = []
    row_parts = []
    for at in range(shard_count):
        part = lax.dynamic_index_in_dim(columns_own, own ^ at, 0, keepdims=False)
        rows = relative[at]
        grad_parts.append(swap(part, "seq", at) if at else part)
        row_parts.append(swap(rows, "seq", at) if at else rows)
    head_order = own ^ jnp.arange(shard_count, dtype=jnp.int32)
    out_grad = (
        jnp.transpose(jnp.stack(grad_parts)[head_order], (0, 2, 1))
        .reshape(shard_count * local_width, -1)
        .astype(jnp.float32)
    )
    returned = jnp.transpose(jnp.stack(row_parts)[head_order], (1, 0, 2)).reshape(shard_rows, -1)
    branch = lax.dot_general(
        returned, out_full, (((1,), (1,)), ((), ())), preferred_element_type=jnp.float32
    )
    ordered = lax.dynamic_slice_in_dim(embedded, own * shard_rows, shard_rows, 0)
    layer_out = (ordered.astype(jnp.float32) + branch).astype(jnp.bfloat16)
    return (layer_out, out_grad)


def solution(mesh):
    placed = (
        P(None, ("dp", "seq")),
        P("dp", None),
        P("dp", None, None),
        P(),
        P(),
        P(),
        P(),
        P(),
        P(),
        P(),
        P(),
        P(None, ("dp", "seq")),
        P(("dp", "seq"), None),
    )
    return jax.shard_map(
        per_device,
        mesh=mesh,
        in_specs=placed,
        out_specs=(P(("dp", "seq"), None), P(None, ("dp", "seq"))),
        check_vma=False,
    )
```
